128 devices in a mesh: dp: 4 (over y), expert: 32 (over z, x, core).
Axes of the slice: x: 4, y: 4, z: 4, core: 2. Of those that a mesh axis runs over, the one named last changes fastest.
Arguments:
- hidden_in: bfloat16 [16384, 2880], P(('dp', 'expert')), may hold values from -6 to 6
- queries: bfloat16 [16384, 4096], P(('dp', 'expert')), may hold values from -50 to 50
- kv_pages: bfloat16 [2048, 128, 1024], P(('dp', 'expert')), may hold values from -4.5 to 4.5
- page_table: int32 [512, 4], P(('dp', 'expert')), may hold values from 0 to 15, as said below
- new_rows: int32 [512], P(('dp', 'expert')), may hold values from 1 to 125, as said below
- context: int32 [512], P(('dp', 'expert')), may hold values from 1 to 512, as said below
- sink_logits: float32 [64], replicated, may hold values from 0 to 8
- out_proj: bfloat16 [4096, 2880], P('dp'), may hold values from -0.09375 to 0.09375
- norm_gain: float32 [2880], replicated, may hold values from 0.1 to 1.9
- routes: int32 [16384, 4], P(('dp', 'expert')), may hold values from 0 to 31, all different within a row; in each aligned block of 128 rows (0 to 127, 128 to 255, ...) at most 20 rows name the same one
- route_weights: float32 [16384, 4], P(('dp', 'expert')), may hold values from 0.05 to 1
- gate_up: bfloat16 [32, 2, 2880, 2048], P('expert', None, None, 'dp'), may hold values from -0.109375 to 0.109375
- down_proj: bfloat16 [32, 2048, 2880], P('expert', 'dp'), may hold values from -0.125 to 0.125
Outputs:
- layer_out: bfloat16 [16384, 2880], P(('dp', 'expert'))
The draws below stay inside these ranges and needn't reach their ends.
Inputs may be any that keep to these rules, and one draw needn't show every extreme that they name: `page_table`: each request's table row lists distinct pages of its own block of 16 pages; each block's table holds each of its page numbers once. The new_rows of one block of 4 requests sum to 128; one to three requests of each block have more than one. new_rows <= context; in every block some request has context 4 * 128. Within the 128 rows of one block, no expert is named by more than 20 routes; some expert reaches 20 in every draw.
All inputs are finite; a program needn't handle non-finite values.
Results may differ from the reference program's by a relative error of at most 0.015.
Values may be sent and summed in bfloat16 or wider, within the bound.
A program may use at most 128 MiB of HBM per device.

```python
import math
import jax
import jax.numpy as jnp
import numpy as np
from jax import lax

D = 2880
QH = 64
KVH = 8
HD = 64
E = 32
TOP = 4
FF = 2048
PAGE = 128
ROWS_DEV = 128
REQ_DEV = 4
PPR = 4
PAGES_DEV = 16
CAP = 20
TOKENS = 16384
REQS = 512
PAGES = 2048
N_DP = 4
N_EXPERT = 32


def layout(key):
    base_key = jax.random.fold_in(key, 9137)
    devices = TOKENS // ROWS_DEV
    key_list = jax.random.split(jax.random.fold_in(base_key, 1), devices)
    order = jax.vmap(lambda one_key: jax.random.permutation(one_key, REQ_DEV))(key_list).astype(jnp.int32)
    prefill_count = jax.random.randint(jax.random.fold_in(base_key, 2), (devices, 1), 1, 4).astype(jnp.int32)
    prefill = order < prefill_count
    share_raw = jax.random.randint(jax.random.fold_in(base_key, 3), (devices, REQ_DEV), 1, 100).astype(jnp.int32)
    share_raw = jnp.where(prefill, share_raw, 0)
    prefill_total = ROWS_DEV - (REQ_DEV - prefill_count)
    spare_rows = prefill_total - prefill_count
    share_rows = jnp.where(prefill, 1 + spare_rows * share_raw // jnp.sum(share_raw, axis=1, keepdims=True), 0)
    left_rows = prefill_total - jnp.sum(share_rows, axis=1, keepdims=True)
    share_rows = share_rows + jnp.where(order == 0, left_rows, 0)
    new_rows = jnp.where(prefill, share_rows, 1).astype(jnp.int32)
    max_context = PPR * PAGE
    extra_rows = jax.random.randint(jax.random.fold_in(base_key, 4), (devices, REQ_DEV), 0, max_context + 1).astype(jnp.int32)
    context = jnp.minimum(new_rows + extra_rows, max_context)
    context = jnp.where(order == REQ_DEV - 1, max_context, context).astype(jnp.int32)
    page_keys = jax.random.split(jax.random.fold_in(base_key, 5), devices)
    pages = jax.vmap(lambda one_key: jax.random.permutation(one_key, PAGES_DEV))(page_keys).astype(jnp.int32)
    return (new_rows, context, pages.reshape(devices, REQ_DEV, PPR))


def draw_page_table(key, part):
    new_rows, context, pages = layout(key)
    return pages.reshape(REQS, PPR)


def draw_new_rows(key, part):
    new_rows, context, pages = layout(key)
    return new_rows.reshape(REQS)


def draw_context(key, part):
    new_rows, context, pages = layout(key)
    return context.reshape(REQS)


def draw_kv_pages(key, part):
    shape = (PAGES * PAGE, KVH, HD)
    keys_f = jnp.clip(jax.random.normal(jax.random.fold_in(key, 21), shape, jnp.float32), -4.5, 4.5)
    vals_f = jnp.clip(jax.random.normal(jax.random.fold_in(key, 22), shape, jnp.float32), -4.5, 4.5)
    stacked = jnp.stack([keys_f, vals_f], axis=2)
    return stacked.reshape(PAGES, PAGE, KVH * 2 * HD).astype(jnp.bfloat16)


def draw_queries(key, part):
    devices = TOKENS // ROWS_DEV
    group_size = QH // KVH
    shape = (devices, ROWS_DEV, KVH, group_size, HD)
    query_f = jnp.clip(1.5 * jax.random.normal(jax.random.fold_in(key, 31), shape, jnp.float32), -9.0, 9.0)
    return query_f.reshape(TOKENS, QH * HD).astype(jnp.bfloat16)


def shard_levels(stream_key, shape, shards, least, high):
    loudness, own = 1.0, jax.random.fold_in(stream_key, 6)
    for axis_at, parts in shards:
        draws = jnp.exp(jax.random.uniform(jax.random.fold_in(own, axis_at), (parts,), jnp.float32, least / len(shards), high / len(shards)))
        loudness = loudness * jnp.repeat(draws, shape[axis_at] // parts).reshape([-1 if axis == axis_at else 1 for axis in range(len(shape))])
    return loudness


def assign_block(rng, own, number, rows, amount, top, bound, skew):
    order = jax.random.permutation(rng, amount)
    heavy_load, usual = portions_of(amount, rows * top, bound, skew, True), portions_of(amount, rows * top, bound, skew, False)
    places = jnp.arange(amount)

    def named(lengths, offset_by):
        used = int((lengths > 0).sum())
        fixed = max(1, used // 4)
        passed = fixed + (places - fixed + offset_by * (used - fixed)) % max(1, amount - fixed)
        return jnp.zeros((amount,), jnp.int32).at[order[jnp.where(places < fixed, places, passed)]].set(jnp.asarray(lengths, jnp.int32))

    lengths = jnp.where(number % 4 == 0, named(heavy_load, number // 4), named(usual, number - number // 4 - 1))
    mixed = jax.random.permutation(jax.random.fold_in(own, 3), amount)
    donor, sink = mixed[0:amount // 2 * 2:2], mixed[1:amount // 2 * 2:2]
    slack = jnp.minimum(lengths[donor] - 1, bound - lengths[sink]) // 2
    slack = jnp.where((donor == order[0]) | (sink == order[0]) | (lengths[sink] == 0), 0, jnp.maximum(slack, 0))
    passed = jax.random.randint(jax.random.fold_in(own, 4), (amount // 2,), 0, 1 << 20) % (slack + 1)
    lengths = lengths.at[donor].add(-passed).at[sink].add(passed)
    labels = jnp.searchsorted(jnp.cumsum(lengths), jnp.arange(rows * top), side="right").astype(jnp.int32)
    listing = labels.reshape(top, rows).T
    listing = listing[jax.random.permutation(jax.random.fold_in(own, 1), rows)]
    offset_by = jax.random.randint(jax.random.fold_in(own, 2), (rows, 1), 0, top)
    return jnp.take_along_axis(listing, (jnp.arange(top)[None, :] + offset_by) % top, axis=1)


def portions_of(amount, total, bound, skew, full):
    portions = [(1 << 20) // math.isqrt(standing ** skew) + 1 for standing in range(1, amount + 1)]
    largest = bound if full else min(bound, max(-(-total // amount), total * portions[0] // sum(portions)))
    least = 1 if total - largest >= amount - 1 else 0
    counts, rest = [largest] + [least] * (amount - 1), total - largest - least * (amount - 1)
    while rest > 0:
        free = [i for i in range(1, amount) if counts[i] < largest] or [i for i in range(1, amount) if counts[i] < bound]
        pool, budget = sum([portions[i] for i in free]), rest
        for i in free:
            extra = min(bound - counts[i], max(1, budget * portions[i] // pool), rest)
            counts[i] = counts[i] + extra
            rest = rest - extra
    return np.array(counts)


def normal_values(stream_key, shape, deviation, most, shards=(), held_as=jnp.bfloat16):
    entries = deviation * jax.random.normal(stream_key, shape, jnp.float32)
    if shards:
        entries = entries * shard_levels(stream_key, shape, shards, -0.22, 0.18)
    return jnp.clip(entries, -most, most).astype(held_as)


def setup_inputs(seed: int = 0) -> dict:
    seeds = jax.random.split(jax.random.key(seed), 14)
    hidden_in = normal_values(seeds[0], (TOKENS, D), 1.0, 6.0, ((0, 128),))
    queries = draw_queries(jax.random.fold_in(seeds[13], 71), 0)
    kv_pages = draw_kv_pages(jax.random.fold_in(seeds[13], 71), 0)
    page_table = draw_page_table(jax.random.fold_in(seeds[13], 71), 0)
    new_rows = draw_new_rows(jax.random.fold_in(seeds[13], 71), 0)
    context = draw_context(jax.random.fold_in(seeds[13], 71), 0)
    sink_logits = jnp.clip(jax.random.uniform(seeds[6], (QH,), jnp.float32, 0.0, 8.0), 0.0, 8.0)
    out_proj = normal_values(seeds[7], (QH * HD, D), (QH * HD) ** -0.5, 0.09375, ((0, 4),))
    norm_gain = jnp.clip(1.0 + 0.18 * jax.random.normal(seeds[8], (D,), jnp.float32), 0.1, 1.9)
    routes_keys = jax.random.split(jax.random.fold_in(seeds[9], 1), TOKENS // ROWS_DEV)
    routes_turns = jax.random.permutation(jax.random.fold_in(seeds[9], 3), TOKENS // ROWS_DEV)
    routes = jax.vmap(lambda own, number: assign_block(jax.random.fold_in(seeds[9], 2), own, number, ROWS_DEV, E, TOP, CAP, 1))(routes_keys, routes_turns).reshape((TOKENS, TOP))
    route_weights = jnp.clip(jnp.exp(math.log(1.0) - 2.9957323 * jax.random.uniform(seeds[10], (TOKENS, TOP), jnp.float32) ** shard_levels(seeds[10], (TOKENS, TOP), ((0, 128),), -0.2, 0.2)), 0.05, 1.0)
    gate_up = normal_values(seeds[11], (E, 2, D, FF), D ** -0.5, 0.109375, ((0, 32), (3, 4)))
    down_proj = normal_values(seeds[12], (E, FF, D), FF ** -0.5, 0.125, ((0, 32), (1, 4)))
    return dict(hidden_in=hidden_in, queries=queries, kv_pages=kv_pages, page_table=page_table, new_rows=new_rows, context=context, sink_logits=sink_logits, out_proj=out_proj, norm_gain=norm_gain, routes=routes, route_weights=route_weights, gate_up=gate_up, down_proj=down_proj)


norm_eps = 1e-05

def rounded(value):
    return lax.optimization_barrier(value.astype(jnp.bfloat16)).astype(jnp.float32)

def attend_device(queries, kv_pages, page_table, new_rows, context, sink_logits):
    row_count = queries.shape[0]
    req_count = new_rows.shape[0]
    req_ends = jnp.cumsum(new_rows).astype(jnp.int32)
    row_index = jnp.arange(row_count, dtype=jnp.int32)
    owner_req = lax.optimization_barrier(jnp.sum((row_index[:, None] >= req_ends[None, :]).astype(jnp.int32), axis=1))
    pick_req = (owner_req[:, None] == jnp.arange(req_count, dtype=jnp.int32)[None, :]).astype(jnp.int32)
    position = row_index + lax.optimization_barrier(jnp.sum(pick_req * (context - req_ends)[None, :], axis=1))
    row_pages = lax.optimization_barrier(jnp.sum(pick_req[:, :, None] * page_table[None, :, :], axis=1)).astype(jnp.int32)
    key_span = row_pages.shape[1] * PAGE
    key_pos = jnp.arange(key_span, dtype=jnp.int32)
    visible = key_pos[None, :] <= position[:, None]
    group_size = QH // KVH

    def one_head(head_idx):
        kv_head = lax.dynamic_slice_in_dim(kv_pages, head_idx * 2 * HD, 2 * HD, 2)
        gathered = kv_head[row_pages].reshape(row_count, key_span, 2 * HD)
        key_part = gathered[:, :, :HD].astype(jnp.float32)
        value_part = gathered[:, :, HD:].astype(jnp.float32)
        query_part = lax.dynamic_slice_in_dim(queries, head_idx * group_size * HD, group_size * HD, 1)
        query_part = query_part.reshape(row_count, group_size, HD).astype(jnp.float32)
        sink_part = lax.dynamic_slice_in_dim(sink_logits, head_idx * group_size, group_size, 0)
        scores = jnp.einsum('rgd,rsd->rgs', query_part, key_part) * (1.0 / math.sqrt(HD))
        scores = jnp.where(visible[:, None, :], scores, -jnp.inf)
        row_max = jnp.maximum(lax.optimization_barrier(jnp.max(scores, axis=2)), sink_part[None, :])
        weight = jnp.exp(scores - row_max[:, :, None])
        denom_sum = lax.optimization_barrier(jnp.sum(weight, axis=2)) + jnp.exp(sink_part[None, :] - row_max)
        probs_bf = rounded(weight / denom_sum[:, :, None])
        return jnp.einsum('rgs,rsd->rgd', probs_bf, value_part).astype(jnp.bfloat16)
    head_parts = lax.map(one_head, jnp.arange(KVH, dtype=jnp.int32))
    return jnp.transpose(head_parts, (1, 0, 2, 3)).reshape(row_count, QH * HD)

def reference(hidden_in, queries, kv_pages, page_table, new_rows, context, sink_logits, out_proj, norm_gain, routes, route_weights, gate_up, down_proj):
    devices = N_DP * N_EXPERT

    def per_device(items):
        return attend_device(items[0], items[1], items[2], items[3], items[4], sink_logits)
    attended = lax.map(per_device, (queries.reshape(devices, ROWS_DEV, QH * HD), kv_pages.reshape(devices, PAGES_DEV, PAGE, KVH * 2 * HD), page_table.reshape(devices, REQ_DEV, PPR), new_rows.reshape(devices, REQ_DEV), context.reshape(devices, REQ_DEV)))
    attended = attended.reshape(TOKENS, QH * HD)
    o_out = jnp.dot(attended, out_proj, preferred_element_type=jnp.float32)
    mixed_f = rounded(hidden_in.astype(jnp.float32) + o_out)
    normed = (mixed_f * lax.rsqrt(lax.optimization_barrier(jnp.mean(mixed_f * mixed_f, axis=1, keepdims=True)) + norm_eps) * norm_gain).astype(jnp.bfloat16)
    assign = routes.reshape(devices, ROWS_DEV * TOP)
    onehot = (assign[:, :, None] == jnp.arange(E, dtype=jnp.int32)[None, None, :]).astype(jnp.int32)
    slot_index = lax.optimization_barrier(jnp.sum((jnp.cumsum(onehot, axis=1) - onehot) * onehot, axis=2)).astype(jnp.int32)
    dev_of = jnp.arange(TOKENS * TOP, dtype=jnp.int32) // (ROWS_DEV * TOP)
    flat_rows = jnp.arange(TOKENS * TOP, dtype=jnp.int32) // TOP
    flat_assign = routes.reshape(-1)
    flat_slot = slot_index.reshape(-1)
    row_table = jnp.full((E, devices, CAP), TOKENS, jnp.int32).at[flat_assign, dev_of, flat_slot].set(flat_rows)
    wgt_table = jnp.zeros((E, devices, CAP), jnp.float32).at[flat_assign, dev_of, flat_slot].set(route_weights.reshape(-1))
    padded = jnp.concatenate([normed, jnp.zeros((1, D), jnp.bfloat16)], axis=0)

    def expert_step(carry, item):
        table_e, wgt_e, gate_up_e, down_e = item
        flat_idx = table_e.reshape(-1)
        picked = padded[flat_idx].astype(jnp.float32)
        gate_up_f = jnp.einsum('cd,tdf->tcf', picked, gate_up_e.astype(jnp.float32))
        gate_f = gate_up_f[0]
        up_f = gate_up_f[1]
        hidden = rounded((up_f + 1.0) * gate_f * jax.nn.sigmoid(1.702 * gate_f))
        quarters = hidden.reshape(hidden.shape[0], N_DP, FF // N_DP)
        down_q = down_e.astype(jnp.float32).reshape(N_DP, FF // N_DP, D)
        partials = rounded(jnp.einsum('cqf,qfd->qcd', quarters, down_q))
        expert_out = lax.optimization_barrier(jnp.sum(partials, axis=0))
        carry = carry.at[flat_idx].add(expert_out * wgt_e.reshape(-1)[:, None])
        return (carry, None)
    expert_mix, _ = lax.scan(expert_step, jnp.zeros((TOKENS + 1, D), jnp.float32), (row_table, wgt_table, gate_up, down_proj))
    return (mixed_f + expert_mix[:TOKENS]).astype(jnp.bfloat16)
```

```python
import math

import jax
import jax.numpy as jnp
from jax import lax
from jax.experimental import pallas as pl
from jax.experimental.pallas import tpu as pltpu
from jax.sharding import PartitionSpec as P

QH = 64
KVH = 8
HD = 64
E = 32
CAP = 20
PAGE = 128
TILE = 16
GROUP = QH // KVH

norm_eps = 1e-05


def attend_kernel(table, new_rows, context, q_ref, kv_ref, sink_ref, out_ref):
    req_count = new_rows.shape[0]
    per_req = table.shape[1]
    lane = lax.broadcasted_iota(jnp.int32, (TILE, 2 * HD), 1)
    low = lane < HD
    sink = sink_ref[0]

    def tile_step(request, start, first_pos, chunk, pages):
        row0 = pl.multiple_of(chunk * TILE, TILE)
        rows = pl.ds(row0, TILE)
        parts = []
        for pair in range(GROUP // 2):
            q = q_ref[rows, pair * 2 * HD : (pair + 1) * 2 * HD].astype(jnp.float32) * (
                1.0 / math.sqrt(HD)
            )
            parts.append(jnp.where(low, q, 0.0))
            parts.append(jnp.where(low, pltpu.roll(q, HD, 1), 0.0))
        q_all = jnp.concatenate(parts, axis=0).astype(jnp.bfloat16)
        kv = jnp.concatenate([kv_ref[table[request, p]] for p in range(pages)], axis=0)
        scores = lax.dot_general(
            q_all, kv, (((1,), (1,)), ((), ())), preferred_element_type=jnp.float32
        )
        span = pages * PAGE
        row_in = lax.rem(lax.broadcasted_iota(jnp.int32, (GROUP * TILE, 1), 0), TILE)
        position = first_pos + (row0 + row_in - start)
        key = lax.broadcasted_iota(jnp.int32, (GROUP * TILE, span), 1)
        scores = jnp.where(key <= position, scores, -jnp.inf)
        row_max = jnp.maximum(jnp.max(scores, axis=1, keepdims=True), sink)
        weight = jnp.exp(scores - row_max)
        denom = jnp.sum(weight, axis=1, keepdims=True) + jnp.exp(sink - row_max)
        probs = (weight * (1.0 / denom)).astype(jnp.bfloat16)
        out = lax.dot_general(
            probs, kv, (((1,), (0,)), ((), ())), preferred_element_type=jnp.float32
        )
        row_id = row0 + lax.broadcasted_iota(jnp.int32, (TILE, 2 * HD), 0)
        mine = (row_id >= start) & (row_id < start + new_rows[request])
        for pair in range(GROUP // 2):
            even = out[2 * pair * TILE : (2 * pair + 1) * TILE]
            odd = out[(2 * pair + 1) * TILE : (2 * pair + 2) * TILE]
            both = jnp.where(low, pltpu.roll(even, HD, 1), odd)
            cols = slice(pair * 2 * HD, (pair + 1) * 2 * HD)
            old = out_ref[rows, cols].astype(jnp.float32)
            out_ref[rows, cols] = jnp.where(mine, both, old).astype(out_ref.dtype)

    start = 0
    for request in range(req_count):
        count = new_rows[request]
        first_pos = context[request] - count

        def body(chunk, carry, request=request, start=start, first_pos=first_pos, count=count):
            last_row = jnp.minimum(chunk * TILE + TILE, start + count) - 1
            pages = (first_pos + last_row - start) // PAGE + 1

            @pl.when(pages <= per_req // 2)
            def _():
                tile_step(request, start, first_pos, chunk, per_req // 2)

            @pl.when(pages > per_req // 2)
            def _():
                tile_step(request, start, first_pos, chunk, per_req)

            return carry

        lax.fori_loop(start // TILE, (start + count - 1) // TILE + 1, body, 0)
        start = start + count


def attend_rows(queries, kv_pages, page_table, new_rows, context, sink_logits):
    row_count = queries.shape[0]
    width = GROUP * HD
    sink_rows = jnp.repeat(sink_logits, TILE).reshape(KVH, GROUP * TILE, 1)
    return pl.pallas_call(
        attend_kernel,
        out_shape=jax.ShapeDtypeStruct(queries.shape, queries.dtype),
        grid_spec=pltpu.PrefetchScalarGridSpec(
            num_scalar_prefetch=3,
            grid=(KVH,),
            in_specs=[
                pl.BlockSpec((row_count, width), lambda h, *_: (0, h)),
                pl.BlockSpec(kv_pages.shape[:2] + (2 * HD,), lambda h, *_: (0, 0, h)),
                pl.BlockSpec((1, GROUP * TILE, 1), lambda h, *_: (h, 0, 0)),
            ],
            out_specs=pl.BlockSpec((row_count, width), lambda h, *_: (0, h)),
        ),
        name="attend",
    )(page_table, new_rows, context, queries, kv_pages, sink_rows)


def expert_terms(gathered_rows, gate_up, down_proj):
    gate_up_f = jnp.einsum("cd,tdf->tcf", gathered_rows, gate_up[0], preferred_element_type=jnp.float32)
    gate_f = gate_up_f[0]
    up_f = gate_up_f[1]
    hidden = ((up_f + 1.0) * gate_f * jax.nn.sigmoid(1.702 * gate_f)).astype(jnp.bfloat16)
    return jnp.dot(hidden, down_proj[0], preferred_element_type=jnp.float32)


def per_device(
    hidden_in,
    queries,
    kv_pages,
    page_table,
    new_rows,
    context,
    sink_logits,
    out_proj,
    norm_gain,
    routes,
    route_weights,
    gate_up,
    down_proj,
):
    row_count = hidden_in.shape[0]
    model_width = hidden_in.shape[1]
    attended = attend_rows(queries, kv_pages, page_table, new_rows, context, sink_logits)
    head_parts = lax.all_to_all(attended, "dp", split_axis=1, concat_axis=0, tiled=True)
    o_out = lax.psum_scatter(
        jnp.dot(head_parts, out_proj, preferred_element_type=jnp.float32).astype(jnp.bfloat16),
        "dp",
        scatter_dimension=0,
        tiled=True,
    ).astype(jnp.float32)
    mixed = (hidden_in.astype(jnp.float32) + o_out).astype(jnp.bfloat16)
    mixed_f = mixed.astype(jnp.float32)
    normed = (
        mixed_f
        * lax.rsqrt(jnp.mean(mixed_f * mixed_f, axis=1, keepdims=True) + norm_eps)
        * norm_gain
    ).astype(jnp.bfloat16)
    expert_ids = jnp.arange(E, dtype=jnp.int32)
    chosen = routes[:, :, None] == expert_ids[None, None, :]
    member = jnp.any(chosen, axis=1)
    order = jnp.arange(row_count, dtype=jnp.int32)
    before = (order[:, None] > order[None, :]).astype(jnp.bfloat16)
    rank = jnp.dot(before, member.astype(jnp.bfloat16), preferred_element_type=jnp.float32)
    rank = jnp.where(member, rank.astype(jnp.int32), -1)
    place = rank[:, :, None] == jnp.arange(CAP, dtype=jnp.int32)[None, None, :]
    weight_of = jnp.sum(jnp.where(chosen, route_weights[:, :, None], 0.0), axis=1)
    place_flat = place.reshape(row_count, E * CAP)
    send_rows = lax.dot_general(
        place_flat.astype(jnp.bfloat16),
        normed,
        (((0,), (0,)), ((), ())),
        preferred_element_type=jnp.float32,
    ).astype(jnp.bfloat16).reshape(E, CAP, model_width)
    spread = jnp.where(place, weight_of[:, :, None], 0.0).reshape(row_count, E * CAP)
    dp_count = lax.axis_size("dp")
    copies = jnp.broadcast_to(send_rows[None], (dp_count,) + send_rows.shape).reshape(
        dp_count * E, CAP, model_width
    )
    gathered_rows = lax.all_to_all(
        copies, ("dp", "expert"), split_axis=0, concat_axis=0, tiled=True
    )
    partials = expert_terms(
        gathered_rows.reshape(-1, model_width), gate_up, down_proj
    ).astype(jnp.bfloat16)
    returned = lax.all_to_all(
        partials.reshape(gathered_rows.shape),
        ("dp", "expert"),
        split_axis=0,
        concat_axis=0,
        tiled=True,
    ).reshape(dp_count * E * CAP, model_width)
    spread_bf = spread.astype(jnp.bfloat16)
    spread_low = (spread - spread_bf.astype(jnp.float32)).astype(jnp.bfloat16)
    expert_mix = jnp.dot(
        jnp.tile(spread_bf, (1, dp_count)), returned, preferred_element_type=jnp.float32
    ) + jnp.dot(jnp.tile(spread_low, (1, dp_count)), returned, preferred_element_type=jnp.float32)
    return (mixed_f + expert_mix).astype(jnp.bfloat16)


def solution(mesh):
    return jax.shard_map(
        per_device,
        mesh=mesh,
        in_specs=(
            P(("dp", "expert"), None),
            P(("dp", "expert"), None),
            P(("dp", "expert"), None, None),
            P(("dp", "expert"), None),
            P(("dp", "expert")),
            P(("dp", "expert")),
            P(),
            P("dp", None),
            P(),
            P(("dp", "expert"), None),
            P(("dp", "expert"), None),
            P("expert", None, None, "dp"),
            P("expert", "dp", None),
        ),
        out_specs=P(("dp", "expert"), None),
        check_vma=False,
    )
```
